256 devices in a mesh: pair: 4 (over y_hi, core), cd: 64 (over z, x, y_lo).
Axes of the slice: x: 4, y: 4 (y_hi: 2, y_lo: 2; y = y_hi * 2 + y_lo), z: 8, core: 2. Of those that a mesh axis runs over, the one named last changes fastest.
Arguments:
- lambda_amps: bfloat16 [11264, 1024], P('pair'), may hold values from -0.0546875 to 0.0546875
- t_amps: bfloat16 [11264, 1024], P('pair', 'cd'), may hold values from -6 to 6
- coef_mu: float32 [768, 64], P('pair'), may hold values from -0.75 to 0.75
- coef_nu: float32 [768, 16], replicated, may hold values from -1.5 to 1.5
Outputs:
- half_ao: bfloat16 [768, 768, 1024], P('pair', 'cd')
The draws below stay inside these ranges and needn't reach their ends.
All inputs are finite; a program needn't handle non-finite values.
Results may differ from the reference program's by a relative error of at most 0.001.
Values sent between devices are 32-bit elements; how exact they have to be, the bound alone decides.
A program may use at most 64 MiB of HBM per device.

```python
import jax
import jax.numpy as jnp
from jax import lax

A = 64
B = 16
NAO = 768
CD = 1024
IJ = 11264


def block_levels(rng, dims, shards, low, top_value):
    def one(axis_at, shards_of):
        draws = jax.random.uniform(jax.random.fold_in(jax.random.fold_in(rng, 6), axis_at), (shards_of,), jnp.float32, low / len(shards), top_value / len(shards))
        return jnp.repeat(jnp.exp(draws), dims[axis_at] // shards_of).reshape((-1,) + (1,) * (len(dims) - axis_at - 1))

    gain = one(*shards[0])
    for cut in shards[1:]:
        gain = gain * one(*cut)
    return gain


def gaussian(own_key, dims, width, limit, split=(), kind=jnp.bfloat16):
    level = block_levels(own_key, dims, split, -0.22, 0.18) if split else 1.0
    array = jax.random.normal(own_key, dims, jnp.float32) * width * level
    return jnp.minimum(jnp.maximum(array, -limit), limit).astype(kind)


def setup_inputs(seed: int = 0) -> dict:
    key_list = jax.random.split(jax.random.key(seed), 5)
    return {
        "lambda_amps": gaussian(key_list[0], (IJ, A * B), IJ ** -0.5, 0.0546875, ((0, 4),)),
        "t_amps": gaussian(key_list[1], (IJ, CD), 1.0, 6.0, ((0, 4), (1, 64))),
        "coef_mu": gaussian(key_list[2], (NAO, A), A ** -0.5, 0.75, ((0, 4),), jnp.float32),
        "coef_nu": gaussian(key_list[3], (NAO, B), B ** -0.5, 1.5, (), jnp.float32),
    }


def reference(lambda_amps, t_amps, coef_mu, coef_nu):
    gamma = lax.dot_general(lambda_amps, t_amps, (((0,), (0,)), ((), ())), preferred_element_type=jnp.float32)
    panel = gamma.reshape(A, B, CD)
    half = jnp.einsum("abc,nb->anc", panel, coef_nu, precision=lax.Precision.HIGHEST)
    blocks = coef_mu.reshape(NAO // 64, 64, A)

    def one_block(rows):
        return jnp.einsum("ma,anc->mnc", rows, half, precision=lax.Precision.HIGHEST).astype(jnp.bfloat16)

    return lax.map(one_block, blocks).reshape(NAO, NAO, CD)
```

```python
import jax
import jax.numpy as jnp
from jax import lax
from jax.experimental import pallas as pl
from jax.experimental.pallas import tpu as pltpu
from jax.sharding import PartitionSpec as P

A = 64
B = 16
NX, NY, NZ = 4, 4, 8
MESH = pl.DeviceIdType.MESH
F32, BF16 = jnp.float32, jnp.bfloat16


class Place:
    def __init__(self):
        pair, cd = lax.axis_index("pair"), lax.axis_index("cd")
        self.core = pair % 2
        self.z = cd // 8
        self.x = (cd // 2) % 4
        self.y = (pair // 2) * 2 + cd % 2
        self.u = self.x + self.core * (self.y - self.x)
        self.v = self.y + self.core * (self.x - self.y)

    def seat(self, core, x, y, z):
        return ((y // 2) * 2 + core, z * 8 + x * 2 + y % 2)

    def far(self, other_core):
        core = (self.core + other_core) % 2
        return self.seat(core, self.x, (self.y + 2) % 4, self.z)

    def partner(self):
        return self.seat(1 - self.core, self.x, self.y, self.z)

    def ring(self, du=0, dv=0, dz=0):
        u, v, z = (self.u + du) % 4, (self.v + dv) % 4, (self.z + dz) % 8
        return self.seat(self.core, u + self.core * (v - u), v + self.core * (u - v), z)


def split(value):
    high = value.astype(BF16)
    return high, (value - high.astype(F32)).astype(BF16)


def gather_kernel(lam_hbm, t_hbm, mu_ref, nu_ref, g_ref, w_ref, m_ref,
                  lam, t_vmem, part, came, lam_sem, t_sem,
                  rs_send, rs_recv, u_send, u_recv, z_send, z_recv, v_send, v_recv, x_send, x_recv):
    me = Place()
    rows = lam_hbm.shape[0]
    pair = lax.axis_index("pair")
    far_same = (pair + 2) % 4
    far_other = ((pair // 2 + 1) % 2) * 2 + 1 - me.core
    near = (pair // 2) * 2 + 1 - me.core
    quarters = [far_same, far_other, near, pair]

    t_copy = pltpu.make_async_copy(t_hbm, t_vmem, t_sem)
    t_copy.start()
    lam_copies = []
    for i, q in enumerate(quarters):
        cols = pl.ds(pl.multiple_of(q * 256, 256), 256)
        copy = pltpu.make_async_copy(lam_hbm.at[:, cols], lam.at[i], lam_sem.at[i])
        copy.start()
        lam_copies.append(copy)

    greeted = [me.far(0), me.far(1), me.partner(), me.ring(du=1), me.ring(du=-1), me.ring(du=2),
               me.ring(dz=1), me.ring(dz=-1), me.ring(dz=2), me.ring(dz=-2), me.ring(dv=1), me.ring(dv=-1)]
    barrier = pltpu.get_barrier_semaphore()
    for peer in greeted:
        pl.semaphore_signal(barrier, inc=1, device_id=peer, device_id_type=MESH)

    sends = []

    def send(src, dst, ssem, rsem, peer):
        copy = pltpu.make_async_remote_copy(src, dst, ssem, rsem, device_id=peer, device_id_type=MESH)
        copy.start()
        sends.append(copy)

    def arrived(dst, ssem, rsem):
        pltpu.make_async_remote_copy(dst, dst, ssem, rsem, device_id=me.partner(), device_id_type=MESH).wait_recv()

    t_copy.wait()
    t_value = t_vmem[...]
    for i in range(4):
        lam_copies[i].wait()
        part[i] = jnp.dot(t_value, lam[i], preferred_element_type=F32)
        if i == 0:
            pl.semaphore_wait(barrier, len(greeted))
        if i < 3:
            peer = (me.far(0), me.far(1), me.partner())[i]
            send(part.at[i], came.at[i], rs_send.at[i], rs_recv.at[i], peer)

    first = lax.axis_index("cd") * 12
    pick = (lax.broadcasted_iota(jnp.int32, (192, 768), 1)
            == first + lax.broadcasted_iota(jnp.int32, (192, 768), 0) // 16).astype(F32).astype(BF16)
    spread = (lax.broadcasted_iota(jnp.int32, (16, 256), 1) % 16
              == lax.broadcasted_iota(jnp.int32, (16, 256), 0)).astype(F32).astype(BF16)
    own_a = (lax.broadcasted_iota(jnp.int32, (192, 256), 1) // 16
             == lax.broadcasted_iota(jnp.int32, (192, 256), 0) % 16)
    for i, term in enumerate(split(nu_ref[...])):
        taken = lax.dot_general(pick, term, (((1,), (1,)), ((), ())), preferred_element_type=F32)
        tiled = jnp.dot(taken.astype(BF16), spread, preferred_element_type=F32)
        w_ref[i] = jnp.where(own_a, tiled, 0.0).astype(BF16)
    mu_value = mu_ref[...]
    mu_high = mu_value.astype(BF16).astype(F32)
    m_ref[...] = jnp.concatenate([mu_high, mu_high, mu_value - mu_high], axis=0).T.astype(BF16)

    for i in range(3):
        arrived(came.at[i], rs_send.at[i], rs_recv.at[i])
    mine = g_ref.at[me.core]
    mine[me.v, me.z, me.u] = (part[3] + came[2]) + (came[0] + came[1])

    u_of = [(me.u + d) % 4 for d in range(4)]
    v_of = [(me.v + d) % 4 for d in range(4)]
    z_of = [(me.z + d) % 8 for d in range(8)]

    def block(dv, dz, du):
        return mine.at[v_of[dv % 4], z_of[dz % 8], u_of[du % 4]]

    def send_u(delta):
        slot = (delta % 4) - 1
        send(block(0, 0, 0), block(0, 0, 0), u_send.at[slot], u_recv.at[slot], me.ring(du=delta))

    def got_u(du):
        slot = (-du % 4) - 1
        arrived(block(0, 0, du), u_send.at[slot], u_recv.at[slot])

    def send_z(du, dz, delta):
        slot = (dz - delta) % 8 - 1
        send(block(0, dz, du), block(0, dz, du), z_send.at[du, slot], z_recv.at[du, slot], me.ring(dz=delta))

    def got_z(du, dz):
        slot = dz % 8 - 1
        arrived(block(0, dz, du), z_send.at[du, slot], z_recv.at[du, slot])

    def unit(dv, dz):
        return mine.at[v_of[dv % 4], z_of[dz % 8]]

    def half(dv, dz, h):
        return mine.at[v_of[dv % 4], z_of[dz % 8], pl.ds(2 * h, 2)]

    def send_v(dz):
        for i, delta in enumerate((1, -1)):
            send(unit(0, dz), unit(0, dz), v_send.at[dz % 8, i], v_recv.at[dz % 8, i], me.ring(dv=delta))

    def got_v(dz, i):
        dv = (-1, 1)[i]
        arrived(unit(dv, dz), v_send.at[dz % 8, i], v_recv.at[dz % 8, i])
        send(half(dv, dz, i), half(dv, dz, i), v_send.at[dz % 8, 2 + i], v_recv.at[dz % 8, 2 + i],
             me.ring(dv=(1, -1)[i]))

    def got_v2(dz):
        for i in range(2):
            arrived(half(2, dz, i), v_send.at[dz % 8, 2 + i], v_recv.at[dz % 8, 2 + i])

    def share(dv, dz):
        send(unit(dv, dz), unit(dv, dz), x_send.at[dv % 4, dz % 8], x_recv.at[dv % 4, dz % 8], me.partner())

    def z_from_origin(du):
        for delta in (2, -2, 1, -1):
            send_z(du, 0, delta)

    def z_take(du, dz):
        got_z(du, dz)
        if dz == -2:
            if du < 2:
                send_z(du, -2, 2)
            send_z(du, -2, 1)
        if dz == 2:
            if du >= 2:
                send_z(du, 2, -2)
            send_z(du, 2, -1)

    def unit_ready(dz):
        send_v(dz)
        share(0, dz)

    def v_take(dz):
        for i in range(2):
            got_v(dz, i)
            share((-1, 1)[i], dz)

    def v2_take(dz):
        got_v2(dz)
        share(2, dz)

    for delta in (2, 1, -1):
        send_u(delta)
    z_from_origin(0)
    for du in (1, 3, 2):
        got_u(du)
        z_from_origin(du)
    unit_ready(0)
    for du in (0, 1, 3, 2):
        for dz in (-2, 2):
            z_take(du, dz)
        for dz in (-1, 1):
            z_take(du, dz)
    for dz in (-2, 2, 1, -1):
        unit_ready(dz)
    v_take(0)
    for du in (0, 1, 3, 2):
        for dz in (-3, 3, 4):
            z_take(du, dz)
    for dz in (4, -3, 3):
        unit_ready(dz)
    for dz in (-2, 2, 1, -1):
        v_take(dz)
    v2_take(0)
    for dz in (4, -3, 3):
        v_take(dz)
    for dz in (-2, 2, 1, -1, 4, -3, 3):
        v2_take(dz)
    theirs = g_ref.at[1 - me.core]
    for dv in range(4):
        for dz in range(8):
            arrived(theirs.at[dv, dz], x_send.at[dv, dz], x_recv.at[dv, dz])
    for copy in sends:
        copy.wait_send()


def transform_kernel(g_ref, w_ref, m_ref, out_ref):
    nt = (((1,), (1,)), ((), ()))
    w_high, w_low = w_ref[0], w_ref[1]
    halves = []
    for p in range(4):
        yh, core = p // 2, p % 2
        pieces = []
        for z in range(g_ref.shape[2]):
            for x in range(NX):
                for yl in range(2):
                    y = 2 * yh + yl
                    pieces.append(g_ref[0, y, z, x] if core == 0 else g_ref[1, x, z, y])
        high, low = split(jnp.concatenate(pieces, axis=0))
        value = lax.dot_general(w_high, high, nt, preferred_element_type=F32)
        value += lax.dot_general(w_high, low, nt, preferred_element_type=F32)
        value += lax.dot_general(w_low, high, nt, preferred_element_type=F32)
        halves.append(value)
    m = m_ref[...]
    for nu in range(12):
        rows = slice(nu * 16, nu * 16 + 16)
        high, low = split(jnp.concatenate([value[rows] for value in halves], axis=0))
        stacked = jnp.concatenate([high, low, high], axis=0)
        out_ref[nu] = jnp.dot(m, stacked, preferred_element_type=F32).astype(BF16)


def body(lambda_amps, t_amps, coef_mu, coef_nu):
    rows = lambda_amps.shape[0]
    any_space = pl.BlockSpec(memory_space=pl.ANY)
    vmem = pl.BlockSpec(memory_space=pltpu.VMEM)
    dma = pltpu.SemaphoreType.DMA
    g, w, m = pl.pallas_call(
        gather_kernel,
        out_shape=(
            jax.ShapeDtypeStruct((2, 4, NZ, 4, 16, 256), F32),
            jax.ShapeDtypeStruct((2, 192, 256), BF16),
            jax.ShapeDtypeStruct((192, 192), BF16),
        ),
        in_specs=[any_space, any_space, vmem, vmem],
        out_specs=(vmem, vmem, vmem),
        scratch_shapes=[
            pltpu.VMEM((4, rows, 256), BF16),
            pltpu.VMEM((16, rows), BF16),
            pltpu.VMEM((4, 16, 256), F32),
            pltpu.VMEM((3, 16, 256), F32),
            dma((4,)), dma,
            dma((3,)), dma((3,)),
            dma((3,)), dma((3,)),
            dma((4, 7)), dma((4, 7)),
            dma((8, 4)), dma((8, 4)),
            dma((4, 8)), dma((4, 8)),
        ],
        compiler_params=pltpu.CompilerParams(collective_id=0, has_side_effects=True),
        name="gather",
    )(lambda_amps, t_amps.T, coef_mu.T, coef_nu.T)
    zt = 2
    out = pl.pallas_call(
        transform_kernel,
        grid=(NZ // zt,),
        out_shape=jax.ShapeDtypeStruct((12, 192, 1024), BF16),
        in_specs=[
            pl.BlockSpec((2, 4, zt, 4, 16, 256), lambda i: (0, 0, i, 0, 0, 0)),
            pl.BlockSpec((2, 192, 256), lambda i: (0, 0, 0)),
            pl.BlockSpec((192, 192), lambda i: (0, 0)),
        ],
        out_specs=pl.BlockSpec((12, 192, zt * 128), lambda i: (0, 0, i)),
        name="transform",
    )(g, w, m)
    return jnp.transpose(out, (1, 0, 2))


def solution(mesh):
    in_specs = (P("pair", None), P("pair", "cd"), P("pair", None), P())
    out_specs = P("pair", "cd", None)
    return jax.shard_map(body, mesh=mesh, in_specs=in_specs, out_specs=out_specs, check_vma=False)
```

```python
import jax
import jax.numpy as jnp
from jax import lax
from jax.experimental import pallas as pl
from jax.experimental.pallas import tpu as pltpu
from jax.sharding import PartitionSpec as P

A = 64
B = 16
NX, NY, NZ = 4, 4, 8
MESH = pl.DeviceIdType.MESH
F32, BF16 = jnp.float32, jnp.bfloat16

PLANE = (
    (3, 0), (0, -1), (0, 1), (1, 0), (2, 0), (0, 2), (0, -2), (1, -1),
    (3, -1), (0, 3), (0, -3), (3, 1), (1, 1), (2, -1), (0, 4), (3, 2),
    (1, 2), (3, -2), (1, -2), (2, 1), (3, 3), (1, 3), (3, -3), (1, -3),
    (2, 2), (2, -2), (3, 4), (1, 4), (2, 3), (2, -3), (2, 4),
)
ALONG_Z = (1, -1, 2, -2, 3, -3, 4)
LAG = 2


class Place:
    def __init__(self):
        pair, cd = lax.axis_index("pair"), lax.axis_index("cd")
        self.core = pair % 2
        self.z = cd // 8
        self.x = (cd // 2) % 4
        self.y = (pair // 2) * 2 + cd % 2
        self.u = self.x + self.core * (self.y - self.x)
        self.v = self.y + self.core * (self.x - self.y)

    def seat(self, core, x, y, z):
        return ((y // 2) * 2 + core, z * 8 + x * 2 + y % 2)

    def far(self, other_core):
        core = (self.core + other_core) % 2
        return self.seat(core, self.x, (self.y + 2) % 4, self.z)

    def partner(self):
        return self.seat(1 - self.core, self.x, self.y, self.z)

    def ring(self, du=0, dv=0, dz=0):
        u, v, z = (self.u + du) % 4, (self.v + dv) % 4, (self.z + dz) % 8
        return self.seat(self.core, u + self.core * (v - u), v + self.core * (u - v), z)


def split(value):
    high = value.astype(BF16)
    return high, (value - high.astype(F32)).astype(BF16)


def gather_kernel(lam_hbm, t_hbm, mu_hbm, nu_hbm, half_ref, m_ref, g_ref, w_ref,
                  lam, t_vmem, mu, nu, part, came, lam_sem, in_sem,
                  rs_send, rs_recv, u_send, u_recv, z_send, z_recv, v_send, v_recv, x_send, x_recv):
    me = Place()
    pair = lax.axis_index("pair")
    far_same = (pair + 2) % 4
    far_other = ((pair // 2 + 1) % 2) * 2 + 1 - me.core
    near = (pair // 2) * 2 + 1 - me.core
    quarters = [far_same, far_other, near, pair]

    inputs = [pltpu.make_async_copy(src, dst, in_sem.at[i])
              for i, (src, dst) in enumerate([(t_hbm, t_vmem), (mu_hbm, mu), (nu_hbm, nu)])]
    inputs[0].start()
    lam_copies = []
    for i, q in enumerate(quarters):
        cols = pl.ds(pl.multiple_of(q * 256, 256), 256)
        copy = pltpu.make_async_copy(lam_hbm.at[:, cols], lam.at[i], lam_sem.at[i])
        lam_copies.append(copy)
        if i < 2:
            copy.start()

    greeted = [me.far(0), me.far(1), me.partner(), me.ring(du=1), me.ring(du=-1), me.ring(du=2),
               *(me.ring(dz=delta) for delta in ALONG_Z), me.ring(dv=1), me.ring(dv=-1), me.ring(dv=2)]
    barrier = pltpu.get_barrier_semaphore()
    for peer in greeted:
        pl.semaphore_signal(barrier, inc=1, device_id=peer, device_id_type=MESH)

    def remote(ref, ssem, rsem, peer):
        return pltpu.make_async_remote_copy(ref, ref, ssem, rsem, device_id=peer, device_id_type=MESH)

    def arrived(ref, ssem, rsem):
        remote(ref, ssem, rsem, me.partner()).wait_recv()

    def sent(ref, ssem, rsem):
        remote(ref, ssem, rsem, me.partner()).wait_send()

    inputs[0].wait()
    t_value = t_vmem[...]
    cut = lam.shape[1] // 512 * 256
    for i in range(4):
        lam_copies[i].wait()
        if i < 2:
            lam_copies[i + 2].start()
        else:
            inputs[i - 1].start()
        part[i] = (jnp.dot(t_value[:, :cut], lam[i, :cut], preferred_element_type=F32)
                   + jnp.dot(t_value[:, cut:], lam[i, cut:], preferred_element_type=F32))
        if i == 0:
            pl.semaphore_wait(barrier, len(greeted))
        if i < 3:
            peer = (me.far(0), me.far(1), me.partner())[i]
            pltpu.make_async_remote_copy(part.at[i], came.at[i], rs_send.at[i], rs_recv.at[i],
                                         device_id=peer, device_id_type=MESH).start()

    for i in range(3):
        arrived(came.at[i], rs_send.at[i], rs_recv.at[i])
    mine = g_ref.at[me.core]
    theirs = g_ref.at[1 - me.core]
    mine[me.v, me.z, me.u] = (part[3] + came[2]) + (came[0] + came[1])

    u_of = [(me.u + d) % 4 for d in range(4)]
    v_of = [(me.v + d) % 4 for d in range(4)]
    z_of = [(me.z + d) % 8 for d in range(8)]

    def block(du, dz, dv):
        return mine.at[v_of[dv % 4], z_of[dz % 8], u_of[du % 4]]

    def z_pass(delta):
        remote(block(0, 0, 0), z_send, z_recv.at[-delta % 8 - 1], me.ring(dz=delta)).start()

    def u_pass(dz, delta):
        remote(block(0, dz, 0), u_send, u_recv.at[dz % 8, -delta % 4 - 1], me.ring(du=delta)).start()

    def v_pass(du, dz, delta):
        remote(block(du, dz, 0), v_send, v_recv.at[dz % 8], me.ring(dv=delta)).start()

    def share(dz, dv):
        unit = mine.at[v_of[dv], z_of[dz % 8]]
        remote(unit, x_send, x_recv.at[dz % 8], me.partner()).start()

    count = [0] * 8

    def have(du, dz):
        for delta in (2, 1, -1):
            v_pass(du, dz, delta)
        count[dz % 8] += 1
        if count[dz % 8] == 4:
            share(dz, 0)

    for delta in ALONG_Z:
        z_pass(delta)
    for delta in (2, 1, -1):
        u_pass(0, delta)
    have(0, 0)

    inputs[1].wait()
    inputs[2].wait()
    first = lax.axis_index("cd") * 12
    pick = (lax.broadcasted_iota(jnp.int32, (192, 768), 1)
            == first + lax.broadcasted_iota(jnp.int32, (192, 768), 0) // 16).astype(F32).astype(BF16)
    spread = (lax.broadcasted_iota(jnp.int32, (16, 256), 1) % 16
              == lax.broadcasted_iota(jnp.int32, (16, 256), 0)).astype(F32).astype(BF16)
    own_a = (lax.broadcasted_iota(jnp.int32, (192, 256), 1) // 16
             == lax.broadcasted_iota(jnp.int32, (192, 256), 0) % 16)
    for i, term in enumerate(split(nu[...])):
        taken = lax.dot_general(pick, term, (((1,), (1,)), ((), ())), preferred_element_type=F32)
        tiled = jnp.dot(taken.astype(BF16), spread, preferred_element_type=F32)
        w_ref[i] = jnp.where(own_a, tiled, 0.0).astype(BF16)
    mu_value = mu[...]
    mu_high = mu_value.astype(BF16).astype(F32)
    m_ref[...] = jnp.concatenate([mu_high, mu_high, mu_value - mu_high], axis=0).T.astype(BF16)

    for du, dz in PLANE:
        if du:
            arrived(block(du, dz, 0), u_send, u_recv.at[dz % 8, du - 1])
        else:
            arrived(block(0, dz, 0), z_send, z_recv.at[dz % 8 - 1])
            for delta in (2, 1, -1):
                u_pass(dz, delta)
        have(du, dz)

    def transform(dz):
        z = z_of[dz % 8]
        arrived(theirs.at[:, z], x_send, x_recv.at[dz % 8])
        columns = pl.ds(pl.multiple_of(z * 128, 128), 128)
        for p in range(4):
            yh, core = p // 2, p % 2
            pieces = [g_ref[core, (2 * yh + yl, x)[core], z, (x, 2 * yh + yl)[core]]
                      for x in range(NX) for yl in range(2)]
            high, low = split(jnp.concatenate(pieces, axis=0))
            both = lax.dot_general(w_ref[...].reshape(384, 256), high, nt, preferred_element_type=F32)
            value = lax.dot_general(w_ref[0], low, nt, preferred_element_type=F32) + both[:192] + both[192:]
            high, low = split(value)
            for nu_at in range(12):
                half_ref[nu_at, pl.ds(16 * p, 16), columns] = high[16 * nu_at:16 * nu_at + 16]
                half_ref[nu_at, pl.ds(16 * p + 64, 16), columns] = low[16 * nu_at:16 * nu_at + 16]

    nt = (((1,), (1,)), ((), ()))
    turns = (0,) + ALONG_Z
    for i, dz in enumerate(turns):
        arrived(mine.at[pl.ds(0, 3), z_of[dz % 8]], v_send, v_recv.at[dz % 8])
        for dv in (1, 3, 2):
            share(dz, dv)
        if i >= LAG:
            transform(turns[i - LAG])
    for dz in turns[8 - LAG:]:
        transform(dz)

    for i in range(3):
        sent(part.at[i], rs_send.at[i], rs_recv.at[i])
    sent(mine.at[0, pl.ds(0, 6)], u_send, rs_recv.at[0])
    sent(mine.at[0, pl.ds(0, 7), 0], z_send, rs_recv.at[0])
    sent(mine.at[pl.ds(0, 3)], v_send, rs_recv.at[0])
    sent(mine, x_send, rs_recv.at[0])


def transform_kernel(half_ref, m_ref, out_hbm, out, out_sem):
    def out_copy(tile, i):
        part = (pl.ds(4 * i, 4), slice(None), pl.ds(pl.multiple_of(tile * 256, 256), 256))
        return pltpu.make_async_copy(out.at[part], out_hbm.at[part], out_sem.at[tile, i])

    def step(tile, _):
        columns = pl.ds(pl.multiple_of(tile * 256, 256), 256)
        for nu in range(12):
            stacked = jnp.concatenate([half_ref[nu, :, columns], half_ref[nu, :64, columns]], axis=0)
            out[nu, :, columns] = jnp.dot(m_ref[...], stacked, preferred_element_type=F32).astype(BF16)
            if nu % 4 == 3:
                out_copy(tile, nu // 4).start()
        return 0

    lax.fori_loop(0, 4, step, 0)
    for tile in range(4):
        for i in range(3):
            out_copy(tile, i).wait()


def body(lambda_amps, t_amps, coef_mu, coef_nu):
    rows = lambda_amps.shape[0]
    hbm = pl.BlockSpec(memory_space=pltpu.HBM)
    vmem = pl.BlockSpec(memory_space=pltpu.VMEM)
    dma = pltpu.SemaphoreType.DMA
    inputs = (lambda_amps, t_amps.T, coef_mu.T, coef_nu.T)
    half, m = pl.pallas_call(
        gather_kernel,
        out_shape=(
            pltpu.VMEM((12, 128, 1024), BF16),
            pltpu.VMEM((192, 192), BF16),
        ),
        in_specs=[hbm] * 4,
        out_specs=(vmem,) * 2,
        scratch_shapes=[
            pltpu.VMEM((2, 4, NZ, 4, 16, 256), F32),
            pltpu.VMEM((2, 192, 256), BF16),
            pltpu.VMEM((4, rows, 256), BF16),
            pltpu.VMEM((16, rows), BF16),
            pltpu.VMEM((64, 192), F32),
            pltpu.VMEM((16, 768), F32),
            pltpu.VMEM((4, 16, 256), F32),
            pltpu.VMEM((3, 16, 256), F32),
            dma((4,)), dma((3,)),
            dma((3,)), dma((3,)),
            dma, dma((8, 3)),
            dma, dma((7,)),
            dma, dma((8,)),
            dma, dma((8,)),
        ],
        compiler_params=pltpu.CompilerParams(collective_id=0, has_side_effects=True, vmem_limit_bytes=20 * 2**20),
        name="gather",
    )(*(pltpu.with_memory_space_constraint(array, pltpu.HBM) for array in inputs))
    half, m = (pltpu.with_memory_space_constraint(array, pltpu.VMEM) for array in (half, m))
    out = pl.pallas_call(
        transform_kernel,
        out_shape=jax.ShapeDtypeStruct((12, 192, 1024), BF16),
        in_specs=[vmem] * 2,
        out_specs=hbm,
        scratch_shapes=[pltpu.VMEM((12, 192, 1024), BF16), dma((4, 3))],
        compiler_params=pltpu.CompilerParams(vmem_limit_bytes=32 * 2**20),
        name="transform",
    )(half, m)
    return jnp.transpose(out, (1, 0, 2))


def solution(mesh):
    in_specs = (P("pair", None), P("pair", "cd"), P("pair", None), P())
    out_specs = P("pair", "cd", None)
    return jax.shard_map(body, mesh=mesh, in_specs=in_specs, out_specs=out_specs, check_vma=False)
```

```python
import jax
import jax.numpy as jnp
from jax import lax
from jax.experimental import pallas as pl
from jax.experimental.pallas import tpu as pltpu
from jax.sharding import PartitionSpec as P

A = 64
B = 16
NX, NY, NZ = 4, 4, 8
MESH = pl.DeviceIdType.MESH
F32, BF16 = jnp.float32, jnp.bfloat16

PLANE = (
    (0, 1), (0, -1), (1, 0), (3, 0), (0, 2), (0, -2), (2, 0), (0, 3),
    (0, -3), (0, 4), (1, 1), (1, -1), (1, 2), (1, -2), (3, 1), (3, -1),
    (3, 2), (3, -2), (2, 1), (2, -1), (2, 2), (2, -2), (1, 3), (3, 3),
    (2, 3), (1, -3), (3, -3), (2, -3), (1, 4), (3, 4), (2, 4),
)

ALONG_Z = (1, -1, 2, -2, 3, -3, 4)
NEAR_Z = (2, -2, 1, -1)
LAG = 2


class Place:
    def __init__(self):
        pair, cd = lax.axis_index("pair"), lax.axis_index("cd")
        self.core = pair % 2
        self.z = cd // 8
        self.x = (cd // 2) % 4
        self.y = (pair // 2) * 2 + cd % 2
        self.u = self.x + self.core * (self.y - self.x)
        self.v = self.y + self.core * (self.x - self.y)

    def seat(self, core, x, y, z):
        return ((y // 2) * 2 + core, z * 8 + x * 2 + y % 2)

    def far(self, other_core):
        core = (self.core + other_core) % 2
        return self.seat(core, self.x, (self.y + 2) % 4, self.z)

    def partner(self):
        return self.seat(1 - self.core, self.x, self.y, self.z)

    def ring(self, du=0, dv=0, dz=0):
        u, v, z = (self.u + du) % 4, (self.v + dv) % 4, (self.z + dz) % 8
        return self.seat(self.core, u + self.core * (v - u), v + self.core * (u - v), z)


def split(value):
    high = value.astype(BF16)
    return high, (value - high.astype(F32)).astype(BF16)


def gather_kernel(lam_hbm, t_hbm, mu_hbm, nu_hbm, half_ref, m_ref, g_ref, w_ref,
                  lam, t_vmem, mu, nu, part, came, lam_sem, in_sem,
                  rs_send, rs_recv, u_send, u_recv, z_send, z_recv, v_send, v_recv, x_send, x_recv):
    me = Place()
    pair = lax.axis_index("pair")
    far_same = (pair + 2) % 4
    far_other = ((pair // 2 + 1) % 2) * 2 + 1 - me.core
    near = (pair // 2) * 2 + 1 - me.core
    quarters = [far_same, far_other, near, pair]

    inputs = [pltpu.make_async_copy(src, dst, in_sem.at[i])
              for i, (src, dst) in enumerate([(t_hbm, t_vmem), (mu_hbm, mu), (nu_hbm, nu)])]
    inputs[0].start()
    lam_copies = []
    for i, q in enumerate(quarters):
        cols = pl.ds(pl.multiple_of(q * 256, 256), 256)
        copy = pltpu.make_async_copy(lam_hbm.at[:, cols], lam.at[i], lam_sem.at[i])
        lam_copies.append(copy)
        if i < 2:
            copy.start()

    greeted = [me.far(0), me.far(1), me.partner(), me.ring(du=1), me.ring(du=-1), me.ring(du=2),
               *(me.ring(dz=delta) for delta in ALONG_Z), me.ring(dv=1), me.ring(dv=-1), me.ring(dv=2)]
    barrier = pltpu.get_barrier_semaphore()
    for peer in greeted:
        pl.semaphore_signal(barrier, inc=1, device_id=peer, device_id_type=MESH)

    def remote(ref, ssem, rsem, peer):
        return pltpu.make_async_remote_copy(ref, ref, ssem, rsem, device_id=peer, device_id_type=MESH)

    def arrived(ref, ssem, rsem):
        remote(ref, ssem, rsem, me.partner()).wait_recv()

    def sent(ref, ssem, rsem):
        remote(ref, ssem, rsem, me.partner()).wait_send()

    inputs[0].wait()
    t_value = t_vmem[...]
    cut = lam.shape[1] // 512 * 256
    for i in range(4):
        lam_copies[i].wait()
        if i < 2:
            lam_copies[i + 2].start()
        else:
            inputs[i - 1].start()
        part[i] = (jnp.dot(t_value[:, :cut], lam[i, :cut], preferred_element_type=F32)
                   + jnp.dot(t_value[:, cut:], lam[i, cut:], preferred_element_type=F32))
        if i == 0:
            pl.semaphore_wait(barrier, len(greeted))
        if i < 3:
            peer = (me.far(0), me.far(1), me.partner())[i]
            pltpu.make_async_remote_copy(part.at[i], came.at[i], rs_send.at[i], rs_recv.at[i],
                                         device_id=peer, device_id_type=MESH).start()

    for i in range(3):
        arrived(came.at[i], rs_send.at[i], rs_recv.at[i])
    mine = g_ref.at[me.core]
    theirs = g_ref.at[1 - me.core]
    mine[me.v, me.z, me.u] = (part[3] + came[2]) + (came[0] + came[1])

    u_of = [(me.u + d) % 4 for d in range(4)]
    v_of = [(me.v + d) % 4 for d in range(4)]
    z_of = [(me.z + d) % 8 for d in range(8)]

    def block(du, dz, dv):
        return mine.at[v_of[dv % 4], z_of[dz % 8], u_of[du % 4]]

    def z_pass(du, delta):
        remote(block(du, 0, 0), z_send.at[min(du, 1)], z_recv.at[du, -delta % 8 - 1], me.ring(dz=delta)).start()

    def u_pass(dz, delta):
        remote(block(0, dz, 0), u_send, u_recv.at[dz % 8, -delta % 4 - 1], me.ring(du=delta)).start()

    def v_pass(du, dz, delta):
        remote(block(du, dz, 0), v_send, v_recv.at[dz % 8], me.ring(dv=delta)).start()

    def share(dz, dv):
        unit = mine.at[v_of[dv], z_of[dz % 8]]
        remote(unit, x_send, x_recv.at[dz % 8], me.partner()).start()

    count = [0] * 8

    def have(du, dz):
        for delta in (2, 1, -1):
            v_pass(du, dz, delta)
        count[dz % 8] += 1
        if count[dz % 8] == 4:
            share(dz, 0)

    for delta in ALONG_Z:
        z_pass(0, delta)
    for delta in (2, 1, -1):
        u_pass(0, delta)
    have(0, 0)

    inputs[1].wait()
    inputs[2].wait()
    first = lax.axis_index("cd") * 12
    pick = (lax.broadcasted_iota(jnp.int32, (192, 768), 1)
            == first + lax.broadcasted_iota(jnp.int32, (192, 768), 0) // 16).astype(F32).astype(BF16)
    spread = (lax.broadcasted_iota(jnp.int32, (16, 256), 1) % 16
              == lax.broadcasted_iota(jnp.int32, (16, 256), 0)).astype(F32).astype(BF16)
    own_a = (lax.broadcasted_iota(jnp.int32, (192, 256), 1) // 16
             == lax.broadcasted_iota(jnp.int32, (192, 256), 0) % 16)
    for i, term in enumerate(split(nu[...])):
        taken = lax.dot_general(pick, term, (((1,), (1,)), ((), ())), preferred_element_type=F32)
        tiled = jnp.dot(taken.astype(BF16), spread, preferred_element_type=F32)
        w_ref[i] = jnp.where(own_a, tiled, 0.0).astype(BF16)
    mu_value = mu[...]
    mu_high = mu_value.astype(BF16).astype(F32)
    m_ref[...] = jnp.concatenate([mu_high, mu_high, mu_value - mu_high], axis=0).T.astype(BF16)

    for du, dz in PLANE:
        if dz == 0 or (du and dz not in NEAR_Z):
            arrived(block(du, dz, 0), u_send, u_recv.at[dz % 8, du - 1])
        else:
            arrived(block(du, dz, 0), z_send.at[0], z_recv.at[du, dz % 8 - 1])
        if dz == 0:
            for delta in NEAR_Z:
                z_pass(du, delta)
        elif du == 0 and dz not in NEAR_Z:
            for delta in (2, 1, -1):
                u_pass(dz, delta)
        have(du, dz)

    def transform(dz):
        z = z_of[dz % 8]
        arrived(theirs.at[:, z], x_send, x_recv.at[dz % 8])
        columns = pl.ds(pl.multiple_of(z * 128, 128), 128)
        for p in range(4):
            yh, core = p // 2, p % 2
            pieces = [g_ref[core, (2 * yh + yl, x)[core], z, (x, 2 * yh + yl)[core]]
                      for x in range(NX) for yl in range(2)]
            high, low = split(jnp.concatenate(pieces, axis=0))
            both = lax.dot_general(w_ref[...].reshape(384, 256), high, nt, preferred_element_type=F32)
            value = lax.dot_general(w_ref[0], low, nt, preferred_element_type=F32) + both[:192] + both[192:]
            high, low = split(value)
            for nu_at in range(12):
                half_ref[nu_at, pl.ds(16 * p, 16), columns] = high[16 * nu_at:16 * nu_at + 16]
                half_ref[nu_at, pl.ds(16 * p + 64, 16), columns] = low[16 * nu_at:16 * nu_at + 16]

    nt = (((1,), (1,)), ((), ()))
    turns = (0,) + ALONG_Z
    for i, dz in enumerate(turns):
        arrived(mine.at[pl.ds(0, 3), z_of[dz % 8]], v_send, v_recv.at[dz % 8])
        for dv in (1, 3, 2):
            share(dz, dv)
        if i >= LAG:
            transform(turns[i - LAG])
    for dz in turns[8 - LAG:]:
        transform(dz)

    for i in range(3):
        sent(part.at[i], rs_send.at[i], rs_recv.at[i])
    sent(mine.at[0, pl.ds(0, 8 - len(NEAR_Z)), pl.ds(0, 3)], u_send, rs_recv.at[0])
    sent(mine.at[0, pl.ds(0, 7), 0], z_send.at[0], rs_recv.at[0])
    sent(mine.at[0, pl.ds(0, len(NEAR_Z)), pl.ds(0, 3)], z_send.at[1], rs_recv.at[0])
    sent(mine.at[pl.ds(0, 3)], v_send, rs_recv.at[0])
    sent(mine, x_send, rs_recv.at[0])


def transform_kernel(half_ref, m_ref, out_hbm, out, out_sem):
    def out_copy(tile, i):
        part = (pl.ds(4 * i, 4), slice(None), pl.ds(pl.multiple_of(tile * 256, 256), 256))
        return pltpu.make_async_copy(out.at[part], out_hbm.at[part], out_sem.at[tile, i])

    def step(tile, _):
        columns = pl.ds(pl.multiple_of(tile * 256, 256), 256)
        for nu in range(12):
            stacked = jnp.concatenate([half_ref[nu, :, columns], half_ref[nu, :64, columns]], axis=0)
            out[nu, :, columns] = jnp.dot(m_ref[...], stacked, preferred_element_type=F32).astype(BF16)
            if nu % 4 == 3:
                out_copy(tile, nu // 4).start()
        return 0

    lax.fori_loop(0, 4, step, 0)
    for tile in range(4):
        for i in range(3):
            out_copy(tile, i).wait()


def body(lambda_amps, t_amps, coef_mu, coef_nu):
    rows = lambda_amps.shape[0]
    hbm = pl.BlockSpec(memory_space=pltpu.HBM)
    vmem = pl.BlockSpec(memory_space=pltpu.VMEM)
    dma = pltpu.SemaphoreType.DMA
    inputs = (lambda_amps, t_amps.T, coef_mu.T, coef_nu.T)
    half, m = pl.pallas_call(
        gather_kernel,
        out_shape=(
            pltpu.VMEM((12, 128, 1024), BF16),
            pltpu.VMEM((192, 192), BF16),
        ),
        in_specs=[hbm] * 4,
        out_specs=(vmem,) * 2,
        scratch_shapes=[
            pltpu.VMEM((2, 4, NZ, 4, 16, 256), F32),
            pltpu.VMEM((2, 192, 256), BF16),
            pltpu.VMEM((4, rows, 256), BF16),
            pltpu.VMEM((16, rows), BF16),
            pltpu.VMEM((64, 192), F32),
            pltpu.VMEM((16, 768), F32),
            pltpu.VMEM((4, 16, 256), F32),
            pltpu.VMEM((3, 16, 256), F32),
            dma((4,)), dma((3,)),
            dma((3,)), dma((3,)),
            dma, dma((8, 3)),
            dma((2,)), dma((4, 7)),
            dma, dma((8,)),
            dma, dma((8,)),
        ],
        compiler_params=pltpu.CompilerParams(collective_id=0, has_side_effects=True, vmem_limit_bytes=20 * 2**20),
        name="gather",
    )(*(pltpu.with_memory_space_constraint(array, pltpu.HBM) for array in inputs))
    half, m = (pltpu.with_memory_space_constraint(array, pltpu.VMEM) for array in (half, m))
    out = pl.pallas_call(
        transform_kernel,
        out_shape=jax.ShapeDtypeStruct((12, 192, 1024), BF16),
        in_specs=[vmem] * 2,
        out_specs=hbm,
        scratch_shapes=[pltpu.VMEM((12, 192, 1024), BF16), dma((4, 3))],
        compiler_params=pltpu.CompilerParams(vmem_limit_bytes=32 * 2**20),
        name="transform",
    )(half, m)
    return jnp.transpose(out, (1, 0, 2))


def solution(mesh):
    in_specs = (P("pair", None), P("pair", "cd"), P("pair", None), P())
    out_specs = P("pair", "cd", None)
    return jax.shard_map(body, mesh=mesh, in_specs=in_specs, out_specs=out_specs, check_vma=False)
```

```python
import jax
import jax.numpy as jnp
from jax import lax
from jax.experimental import pallas as pl
from jax.experimental.pallas import tpu as pltpu
from jax.sharding import PartitionSpec as P

A = 64
B = 16
NX, NY, NZ = 4, 4, 8
MESH = pl.DeviceIdType.MESH
F32, BF16 = jnp.float32, jnp.bfloat16

PLANE = (
    (0, 1), (0, -1), (1, 0), (3, 0), (0, 2), (0, -2), (2, 0), (0, 3),
    (0, -3), (0, 4), (1, 1), (1, -1), (1, 2), (1, -2), (3, 1), (3, -1),
    (3, 2), (3, -2), (2, 1), (2, -1), (2, 2), (2, -2), (1, 3), (3, 3),
    (2, 3), (1, -3), (3, -3), (2, -3), (1, 4), (3, 4), (2, 4),
)

ALONG_Z = (1, -1, 2, -2, 3, -3, 4)
NEAR_Z = (1, -1, 2, -2)
LAG = 2


class Place:
    def __init__(self):
        pair, cd = lax.axis_index("pair"), lax.axis_index("cd")
        self.core = pair % 2
        self.z = cd // 8
        self.x = (cd // 2) % 4
        self.y = (pair // 2) * 2 + cd % 2
        self.u = self.x + self.core * (self.y - self.x)
        self.v = self.y + self.core * (self.x - self.y)

    def seat(self, core, x, y, z):
        return ((y // 2) * 2 + core, z * 8 + x * 2 + y % 2)

    def far(self, other_core):
        core = (self.core + other_core) % 2
        return self.seat(core, self.x, (self.y + 2) % 4, self.z)

    def partner(self):
        return self.seat(1 - self.core, self.x, self.y, self.z)

    def ring(self, du=0, dv=0, dz=0):
        u, v, z = (self.u + du) % 4, (self.v + dv) % 4, (self.z + dz) % 8
        return self.seat(self.core, u + self.core * (v - u), v + self.core * (u - v), z)


def split(value):
    high = value.astype(BF16)
    return high, (value - high.astype(F32)).astype(BF16)


def gather_kernel(lam_hbm, t_hbm, mu_hbm, nu_hbm, half_ref, m_ref, g_ref, w_ref,
                  lam, t_vmem, mu, nu, part, came, lam_sem, in_sem,
                  rs_send, rs_recv, u_send, u_recv, z_send, z_recv, v_send, v_recv, x_send, x_recv):
    me = Place()
    pair = lax.axis_index("pair")
    far_same = (pair + 2) % 4
    far_other = ((pair // 2 + 1) % 2) * 2 + 1 - me.core
    near = (pair // 2) * 2 + 1 - me.core
    quarters = [far_same, far_other, near, pair]

    inputs = [pltpu.make_async_copy(src, dst, in_sem.at[i])
              for i, (src, dst) in enumerate([(t_hbm, t_vmem), (mu_hbm, mu), (nu_hbm, nu)])]
    inputs[0].start()
    lam_copies = []
    for i, q in enumerate(quarters):
        cols = pl.ds(pl.multiple_of(q * 256, 256), 256)
        copy = pltpu.make_async_copy(lam_hbm.at[:, cols], lam.at[i], lam_sem.at[i])
        lam_copies.append(copy)
        if i < 2:
            copy.start()

    greeted = [me.far(0), me.far(1), me.partner(), me.ring(du=1), me.ring(du=-1), me.ring(du=2),
               *(me.ring(dz=delta) for delta in ALONG_Z), me.ring(dv=1), me.ring(dv=-1), me.ring(dv=2)]
    barrier = pltpu.get_barrier_semaphore()
    for peer in greeted:
        pl.semaphore_signal(barrier, inc=1, device_id=peer, device_id_type=MESH)

    def remote(ref, ssem, rsem, peer):
        return pltpu.make_async_remote_copy(ref, ref, ssem, rsem, device_id=peer, device_id_type=MESH)

    def arrived(ref, ssem, rsem):
        remote(ref, ssem, rsem, me.partner()).wait_recv()

    def sent(ref, ssem, rsem):
        remote(ref, ssem, rsem, me.partner()).wait_send()

    inputs[0].wait()
    t_value = t_vmem[...]
    cut = lam.shape[1] // 512 * 256
    for i in range(4):
        lam_copies[i].wait()
        if i < 2:
            lam_copies[i + 2].start()
        else:
            inputs[i - 1].start()
        part[i] = (jnp.dot(t_value[:, :cut], lam[i, :cut], preferred_element_type=F32)
                   + jnp.dot(t_value[:, cut:], lam[i, cut:], preferred_element_type=F32))
        if i == 0:
            pl.semaphore_wait(barrier, len(greeted))
        if i < 3:
            peer = (me.far(0), me.far(1), me.partner())[i]
            pltpu.make_async_remote_copy(part.at[i], came.at[i], rs_send.at[i], rs_recv.at[i],
                                         device_id=peer, device_id_type=MESH).start()

    for i in range(3):
        arrived(came.at[i], rs_send.at[i], rs_recv.at[i])
    mine = g_ref.at[me.core]
    theirs = g_ref.at[1 - me.core]
    mine[me.v, me.z, me.u] = (part[3] + came[2]) + (came[0] + came[1])

    u_of = [(me.u + d) % 4 for d in range(4)]
    v_of = [(me.v + d) % 4 for d in range(4)]
    z_of = [(me.z + d) % 8 for d in range(8)]

    def block(du, dz, dv):
        return mine.at[v_of[dv % 4], z_of[dz % 8], u_of[du % 4]]

    def z_pass(du, delta):
        remote(block(du, 0, 0), z_send.at[min(du, 1)], z_recv.at[du, -delta % 8 - 1], me.ring(dz=delta)).start()

    def u_pass(dz, delta):
        remote(block(0, dz, 0), u_send, u_recv.at[dz % 8, -delta % 4 - 1], me.ring(du=delta)).start()

    def v_pass(du, dz, delta):
        remote(block(du, dz, 0), v_send, v_recv.at[dz % 8], me.ring(dv=delta)).start()

    def share(dz, dv):
        unit = mine.at[v_of[dv], z_of[dz % 8]]
        remote(unit, x_send, x_recv.at[dz % 8], me.partner()).start()

    count = [0] * 8

    def have(du, dz):
        for delta in (2, 1, -1):
            v_pass(du, dz, delta)
        count[dz % 8] += 1
        if count[dz % 8] == 4:
            share(dz, 0)

    for delta in ALONG_Z:
        z_pass(0, delta)
    for delta in (2, 1, -1):
        u_pass(0, delta)
    have(0, 0)

    inputs[1].wait()
    inputs[2].wait()
    first = lax.axis_index("cd") * 12
    pick = (lax.broadcasted_iota(jnp.int32, (192, 768), 1)
            == first + lax.broadcasted_iota(jnp.int32, (192, 768), 0) // 16).astype(F32).astype(BF16)
    spread = (lax.broadcasted_iota(jnp.int32, (16, 256), 1) % 16
              == lax.broadcasted_iota(jnp.int32, (16, 256), 0)).astype(F32).astype(BF16)
    own_a = (lax.broadcasted_iota(jnp.int32, (192, 256), 1) // 16
             == lax.broadcasted_iota(jnp.int32, (192, 256), 0) % 16)
    for i, term in enumerate(split(nu[...])):
        taken = lax.dot_general(pick, term, (((1,), (1,)), ((), ())), preferred_element_type=F32)
        tiled = jnp.dot(taken.astype(BF16), spread, preferred_element_type=F32)
        w_ref[i] = jnp.where(own_a, tiled, 0.0).astype(BF16)
    mu_value = mu[...]
    mu_high = mu_value.astype(BF16).astype(F32)
    m_ref[...] = jnp.concatenate([mu_high, mu_high, mu_value - mu_high], axis=0).T.astype(BF16)

    for du, dz in PLANE:
        if dz == 0 or (du and dz not in NEAR_Z):
            arrived(block(du, dz, 0), u_send, u_recv.at[dz % 8, du - 1])
        else:
            arrived(block(du, dz, 0), z_send.at[0], z_recv.at[du, dz % 8 - 1])
        if dz == 0:
            for delta in NEAR_Z:
                z_pass(du, delta)
        elif du == 0 and dz not in NEAR_Z:
            for delta in (2, 1, -1):
                u_pass(dz, delta)
        have(du, dz)

    def transform(dz):
        z = z_of[dz % 8]
        arrived(theirs.at[:, z], x_send, x_recv.at[dz % 8])
        columns = pl.ds(pl.multiple_of(z * 128, 128), 128)
        for p in range(4):
            yh, core = p // 2, p % 2
            pieces = [g_ref[core, (2 * yh + yl, x)[core], z, (x, 2 * yh + yl)[core]]
                      for x in range(NX) for yl in range(2)]
            high, low = split(jnp.concatenate(pieces, axis=0))
            both = lax.dot_general(w_ref[...].reshape(384, 256), high, nt, preferred_element_type=F32)
            value = lax.dot_general(w_ref[0], low, nt, preferred_element_type=F32) + both[:192] + both[192:]
            high, low = split(value)
            for nu_at in range(12):
                half_ref[nu_at, pl.ds(16 * p, 16), columns] = high[16 * nu_at:16 * nu_at + 16]
                half_ref[nu_at, pl.ds(16 * p + 64, 16), columns] = low[16 * nu_at:16 * nu_at + 16]

    nt = (((1,), (1,)), ((), ()))
    turns = (0,) + ALONG_Z
    for i, dz in enumerate(turns):
        arrived(mine.at[pl.ds(0, 3), z_of[dz % 8]], v_send, v_recv.at[dz % 8])
        for dv in (1, 3, 2):
            share(dz, dv)
        if i >= LAG:
            transform(turns[i - LAG])
    for dz in turns[8 - LAG:]:
        transform(dz)

    for i in range(3):
        sent(part.at[i], rs_send.at[i], rs_recv.at[i])
    sent(mine.at[0, pl.ds(0, 8 - len(NEAR_Z)), pl.ds(0, 3)], u_send, rs_recv.at[0])
    sent(mine.at[0, pl.ds(0, 7), 0], z_send.at[0], rs_recv.at[0])
    sent(mine.at[0, pl.ds(0, len(NEAR_Z)), pl.ds(0, 3)], z_send.at[1], rs_recv.at[0])
    sent(mine.at[pl.ds(0, 3)], v_send, rs_recv.at[0])
    sent(mine, x_send, rs_recv.at[0])


def transform_kernel(half_ref, m_ref, out_hbm, out, out_sem):
    def out_copy(tile, i):
        part = (pl.ds(2 * i, 2), slice(None), pl.ds(pl.multiple_of(tile * 256, 256), 256))
        return pltpu.make_async_copy(out.at[part], out_hbm.at[part], out_sem.at[tile, i])

    def step(tile, _):
        columns = pl.ds(pl.multiple_of(tile * 256, 256), 256)
        for nu in range(12):
            stacked = jnp.concatenate([half_ref[nu, :, columns], half_ref[nu, :64, columns]], axis=0)
            out[nu, :, columns] = jnp.dot(m_ref[...], stacked, preferred_element_type=F32).astype(BF16)
            if nu % 2 == 1:
                out_copy(tile, nu // 2).start()
        return 0

    lax.fori_loop(0, 4, step, 0)
    for tile in range(4):
        for i in range(6):
            out_copy(tile, i).wait()


def body(lambda_amps, t_amps, coef_mu, coef_nu):
    rows = lambda_amps.shape[0]
    hbm = pl.BlockSpec(memory_space=pltpu.HBM)
    vmem = pl.BlockSpec(memory_space=pltpu.VMEM)
    dma = pltpu.SemaphoreType.DMA
    inputs = (lambda_amps, t_amps.T, coef_mu.T, coef_nu.T)
    half, m = pl.pallas_call(
        gather_kernel,
        out_shape=(
            pltpu.VMEM((12, 128, 1024), BF16),
            pltpu.VMEM((192, 192), BF16),
        ),
        in_specs=[hbm] * 4,
        out_specs=(vmem,) * 2,
        scratch_shapes=[
            pltpu.VMEM((2, 4, NZ, 4, 16, 256), F32),
            pltpu.VMEM((2, 192, 256), BF16),
            pltpu.VMEM((4, rows, 256), BF16),
            pltpu.VMEM((16, rows), BF16),
            pltpu.VMEM((64, 192), F32),
            pltpu.VMEM((16, 768), F32),
            pltpu.VMEM((4, 16, 256), F32),
            pltpu.VMEM((3, 16, 256), F32),
            dma((4,)), dma((3,)),
            dma((3,)), dma((3,)),
            dma, dma((8, 3)),
            dma((2,)), dma((4, 7)),
            dma, dma((8,)),
            dma, dma((8,)),
        ],
        compiler_params=pltpu.CompilerParams(collective_id=0, has_side_effects=True, vmem_limit_bytes=20 * 2**20),
        name="gather",
    )(*(pltpu.with_memory_space_constraint(array, pltpu.HBM) for array in inputs))
    half, m = (pltpu.with_memory_space_constraint(array, pltpu.VMEM) for array in (half, m))
    out = pl.pallas_call(
        transform_kernel,
        out_shape=jax.ShapeDtypeStruct((12, 192, 1024), BF16),
        in_specs=[vmem] * 2,
        out_specs=hbm,
        scratch_shapes=[pltpu.VMEM((12, 192, 1024), BF16), dma((4, 6))],
        compiler_params=pltpu.CompilerParams(vmem_limit_bytes=32 * 2**20),
        name="transform",
    )(half, m)
    return jnp.transpose(out, (1, 0, 2))


def solution(mesh):
    in_specs = (P("pair", None), P("pair", "cd"), P("pair", None), P())
    out_specs = P("pair", "cd", None)
    return jax.shard_map(body, mesh=mesh, in_specs=in_specs, out_specs=out_specs, check_vma=False)
```
